128 devices in a mesh: ctx: 32 (over z, x, core), exp: 4 (over y).
Axes of the slice: x: 4, y: 4, z: 4, core: 2. Of those that a mesh axis runs over, the one named last changes fastest.
Arguments:
- stored: bfloat16 [4, 16384, 2048], P(None, 'ctx'), may hold values from -50 to 50
- depth_weights: float32 [4], replicated, may hold values from 0.2 to 1
- attn_gain: float32 [2048], replicated, may hold values from 0.5 to 1.5
- qkv_proj: bfloat16 [2048, 3, 16, 128], P(None, None, 'exp'), may hold values from -0.125 to 0.125
- q_gain: float32 [16, 128], P('exp'), may hold values from 1 to 2.5
- k_gain: float32 [16, 128], P('exp'), may hold values from 1 to 2.5
- out_proj: bfloat16 [2048, 2048], P('exp'), may hold values from -0.5 to 0.5
- moe_gain: float32 [2048], replicated, may hold values from 0.5 to 1.5
- router: bfloat16 [2048, 64], replicated, may hold values from -0.125 to 0.125
- gate_proj: bfloat16 [2048, 90112], P(None, ('ctx', 'exp')), may hold values from -0.125 to 0.125
- up_proj: bfloat16 [2048, 90112], P(None, ('ctx', 'exp')), may hold values from -0.125 to 0.125
- down_proj: bfloat16 [90112, 2048], P(('ctx', 'exp')), may hold values from -0.15625 to 0.15625
- expert_ids: int32 [16384, 6], P(('ctx', 'exp')), may hold values from 0 to 63, all different within a row; in each aligned block of 128 rows (0 to 127, 128 to 255, ...) at most 16 rows name the same one
- block_pattern: int32 [16, 256, 8], replicated, may hold values from -1 to 255, as said below
Outputs:
- layer_out: bfloat16 [16384, 2048], P(('ctx', 'exp'))
The draws below stay inside these ranges and needn't reach their ends.
Inputs may be any that keep to these rules, and one draw needn't show every extreme that they name: `expert_ids`: each row names 6 different experts; among the 128 rows of one device no expert is named by more than 16 rows, and some device reaches 16. Entry 0 of block_pattern[h, b] is b; the other 7 entries are distinct blocks before b, or -1 where fewer blocks precede b.
All inputs are finite; a program needn't handle non-finite values.
Results may differ from the reference program's by a relative error of at most 0.015.
Values may be sent and summed in bfloat16 or wider, within the bound.
No kernel may reach another device: no remote copies, remote signals or barrier semaphores. Data moves between devices by JAX's collectives and lax.ppermute only.
A program may use at most 128 MiB of HBM per device.

```python
import math
import jax
import jax.numpy as jnp
import numpy as np
from jax import lax

D = 2048
HEADS = 16
DH = 128
FF = 1408
TOPK = 6
DEPTH = 4
BLK = 64
KL = 8
TOK = 128
EXPERTS = 64
SEQ = 16384
NB = 256
CAP = 16
N_CTX = 32
N_EXP = 4


def draw_stored(key, part):
    first, second, third = jax.random.split(key, 3)
    shape = (DEPTH, SEQ, D)
    row_scale = jnp.exp(jax.random.uniform(second, (DEPTH, SEQ, 1), jnp.float32, -1.15, 1.15))
    col_scale = jnp.exp(jax.random.uniform(third, (1, 1, D), jnp.float32, -1.15, 1.15))
    base = jnp.clip(jax.random.normal(first, shape, jnp.float32), -5.0, 5.0)
    return (base * row_scale * col_scale).astype(jnp.bfloat16)


def draw_block_pattern(key, part):
    shape = (HEADS, NB, NB)
    columns = lax.broadcasted_iota(jnp.int32, shape, 2)
    rows = lax.broadcasted_iota(jnp.int32, shape, 1)
    scores = jax.random.randint(key, shape, 0, 4096, jnp.int32) * NB + columns
    scores = jnp.where(columns < rows, scores, -1)
    top_vals, top_idx = lax.top_k(scores, KL - 1)
    picked = jnp.where(top_vals >= 0, top_idx, -1).astype(jnp.int32)
    own = lax.broadcasted_iota(jnp.int32, (HEADS, NB, 1), 1)
    return jnp.concatenate([own, picked], axis=2)


def block_levels(key, extent, pieces, smallest, top_value):
    gain = 1.0
    for dim, blocks in pieces:
        steps = jax.random.uniform(jax.random.fold_in(jax.random.fold_in(key, 6), dim), (blocks,), jnp.float32, smallest / len(pieces), top_value / len(pieces))
        gain = gain * jnp.repeat(jnp.exp(steps), extent[dim] // blocks).reshape((-1,) + (1,) * (len(extent) - 1 - dim))
    return gain


def deal_out(own_key, own, number, rows, number_of, top, limit, slope):
    sequence = jax.random.permutation(own_key, number_of)
    packed, usual = shares(number_of, rows * top, limit, slope, True), shares(number_of, rows * top, limit, slope, False)
    places = jnp.arange(number_of)

    def named(lengths, rotation):
        used = int((lengths > 0).sum())
        fixed = max(1, used // 4)
        passed = fixed + (places - fixed + rotation * (used - fixed)) % max(1, number_of - fixed)
        return jnp.zeros((number_of,), jnp.int32).at[sequence[jnp.where(places < fixed, places, passed)]].set(jnp.asarray(lengths, jnp.int32))

    lengths = jnp.where(number % 4 == 0, named(packed, number // 4), named(usual, number - number // 4 - 1))
    mixed = jax.random.permutation(jax.random.fold_in(own, 3), number_of)
    donor, receiver = mixed[0:number_of // 2 * 2:2], mixed[1:number_of // 2 * 2:2]
    margin = jnp.minimum(lengths[donor] - 1, limit - lengths[receiver]) // 2
    margin = jnp.where((donor == sequence[0]) | (receiver == sequence[0]) | (lengths[receiver] == 0), 0, jnp.maximum(margin, 0))
    passed = jax.random.randint(jax.random.fold_in(own, 4), (number_of // 2,), 0, 1 << 20) % (margin + 1)
    lengths = lengths.at[donor].add(-passed).at[receiver].add(passed)
    members = jnp.searchsorted(jnp.cumsum(lengths), jnp.arange(rows * top), side="right").astype(jnp.int32)
    grid = members.reshape(top, rows).T
    grid = grid[jax.random.permutation(jax.random.fold_in(own, 1), rows)]
    rotation = jax.random.randint(jax.random.fold_in(own, 2), (rows, 1), 0, top)
    return jnp.take_along_axis(grid, (jnp.arange(top)[None, :] + rotation) % top, axis=1)


def shares(count, total, reach, slope, full):
    weights = [(1 << 20) // math.isqrt(rank ** slope) + 1 for rank in range(1, count + 1)]
    largest = reach if full else min(reach, max(-(-total // count), total * weights[0] // sum(weights)))
    least = 1 if total - largest >= count - 1 else 0
    counts, spare = [largest] + [least] * (count - 1), total - largest - least * (count - 1)
    while spare > 0:
        free = [i for i in range(1, count) if counts[i] < largest] or [i for i in range(1, count) if counts[i] < reach]
        whole, remaining = sum([weights[i] for i in free]), spare
        for i in free:
            more = min(reach - counts[i], max(1, remaining * weights[i] // whole), spare)
            counts[i] = counts[i] + more
            spare = spare - more
    return np.array(counts)


def scatter_about(stream_key, shape, deviation, reach, cuts=(), dtype=jnp.bfloat16):
    gain = block_levels(stream_key, shape, cuts, -0.22, 0.18) if cuts else 1.0
    array = jax.random.normal(stream_key, shape, jnp.float32) * deviation * gain
    return jnp.minimum(jnp.maximum(array, -reach), reach).astype(dtype)


def setup_inputs(seed: int = 0) -> dict:
    seeds = jax.random.split(jax.random.key(seed), 15)
    stored = draw_stored(jax.random.fold_in(seeds[14], 71), 0)
    depth_weights = jnp.clip(jax.random.uniform(seeds[1], (DEPTH,), jnp.float32, 0.2, 1.0), 0.2, 1.0)
    attn_gain = jnp.clip(1.0 + 0.1 * jax.random.normal(seeds[2], (D,), jnp.float32), 0.5, 1.5)
    qkv_proj = scatter_about(seeds[3], (D, 3, HEADS, DH), D ** -0.5, 0.125, ((2, 4),))
    q_gain = jnp.clip(jnp.exp(math.log(2.5) - 0.916290732 * jax.random.uniform(seeds[4], (HEADS, DH), jnp.float32) ** block_levels(seeds[4], (HEADS, DH), ((0, 4),), -0.2, 0.2)), 1.0, 2.5)
    k_gain = jnp.clip(jnp.exp(math.log(2.5) - 0.916290732 * jax.random.uniform(seeds[5], (HEADS, DH), jnp.float32) ** block_levels(seeds[5], (HEADS, DH), ((0, 4),), -0.2, 0.2)), 1.0, 2.5)
    out_proj = scatter_about(seeds[6], (HEADS * DH, D), DH ** -0.5, 0.5, ((0, 4),))
    moe_gain = jnp.clip(1.0 + 0.1 * jax.random.normal(seeds[7], (D,), jnp.float32), 0.5, 1.5)
    router = scatter_about(seeds[8], (D, EXPERTS), D ** -0.5, 0.125)
    gate_proj = scatter_about(seeds[9], (D, EXPERTS * FF), D ** -0.5, 0.125, ((1, 128),))
    up_proj = scatter_about(seeds[10], (D, EXPERTS * FF), D ** -0.5, 0.125, ((1, 128),))
    down_proj = scatter_about(seeds[11], (EXPERTS * FF, D), FF ** -0.5, 0.15625, ((0, 128),))
    expert_ids_keys = jax.random.split(jax.random.fold_in(seeds[12], 1), SEQ // TOK)
    expert_ids_turns = jax.random.permutation(jax.random.fold_in(seeds[12], 3), SEQ // TOK)
    expert_ids = jax.vmap(lambda own, number: deal_out(jax.random.fold_in(seeds[12], 2), own, number, TOK, EXPERTS, TOPK, CAP, 2))(expert_ids_keys, expert_ids_turns).reshape((SEQ, TOPK))
    block_pattern = draw_block_pattern(jax.random.fold_in(seeds[14], 71), 0)
    return {"stored": stored, "depth_weights": depth_weights, "attn_gain": attn_gain, "qkv_proj": qkv_proj, "q_gain": q_gain, "k_gain": k_gain, "out_proj": out_proj, "moe_gain": moe_gain, "router": router, "gate_proj": gate_proj, "up_proj": up_proj, "down_proj": down_proj, "expert_ids": expert_ids, "block_pattern": block_pattern}


EPSILON = 1e-06

def rms_scale(values, gain_vec):
    mean_sq = lax.optimization_barrier(jnp.mean(values * values, axis=-1, keepdims=True))
    return values * lax.rsqrt(mean_sq + EPSILON) * gain_vec

def attend_blocks(q_blocks, key_blocks, value_blocks, pattern_rows, block_ids):
    listed = pattern_rows >= 0
    safe_ids = jnp.maximum(pattern_rows, 0)
    key_sel = jnp.take(key_blocks, safe_ids, axis=0)
    value_sel = jnp.take(value_blocks, safe_ids, axis=0)
    score_scale = q_blocks.shape[-1] ** (-0.5)
    scores = jnp.einsum('nid,nkjd->nikj', q_blocks.astype(jnp.float32), key_sel.astype(jnp.float32)) * score_scale
    diagonal = pattern_rows == block_ids[:, None]
    row_pos = lax.broadcasted_iota(jnp.int32, scores.shape, 1)
    col_pos = lax.broadcasted_iota(jnp.int32, scores.shape, 3)
    visible = listed[:, None, :, None] & (~diagonal[:, None, :, None] | (col_pos <= row_pos))
    weights = jnp.where(visible, jnp.exp(scores), jnp.float32(0.0))
    totals = lax.optimization_barrier(jnp.sum(weights, axis=(2, 3)))
    rounded = weights.astype(jnp.bfloat16).astype(jnp.float32)
    summed = jnp.einsum('nikj,nkjd->nid', rounded, value_sel.astype(jnp.float32))
    return (summed / totals[..., None]).astype(jnp.bfloat16)

def reference(stored, depth_weights, attn_gain, qkv_proj, q_gain, k_gain, out_proj, moe_gain, router, gate_proj, up_proj, down_proj, expert_ids, block_pattern):
    blended = depth_weights[0] * stored[0].astype(jnp.float32)
    for depth_step in range(1, DEPTH):
        blended = blended + depth_weights[depth_step] * stored[depth_step].astype(jnp.float32)
    inputs = blended.astype(jnp.bfloat16)
    normed = rms_scale(inputs.astype(jnp.float32), attn_gain).astype(jnp.bfloat16)
    projected = jnp.dot(normed, qkv_proj.reshape(D, 3 * HEADS * DH), preferred_element_type=jnp.float32)
    projected = projected.reshape(SEQ, 3, HEADS, DH)
    queries = rms_scale(projected[:, 0], q_gain).astype(jnp.bfloat16)
    key_heads = rms_scale(projected[:, 1], k_gain).astype(jnp.bfloat16)
    value_heads = projected[:, 2].astype(jnp.bfloat16)
    q_all = jnp.transpose(queries, (1, 0, 2)).reshape(HEADS, NB, BLK, DH)
    k_all = jnp.transpose(key_heads, (1, 0, 2)).reshape(HEADS, NB, BLK, DH)
    v_all = jnp.transpose(value_heads, (1, 0, 2)).reshape(HEADS, NB, BLK, DH)
    block_ids = jnp.arange(NB).astype(jnp.int32)

    def attend_head(operands):
        q_one, k_one, v_one, pattern_one = operands
        return attend_blocks(q_one, k_one, v_one, pattern_one, block_ids)
    attended = lax.map(attend_head, (q_all, k_all, v_all, block_pattern))
    attended = jnp.transpose(attended.reshape(HEADS, SEQ, DH), (1, 0, 2)).reshape(SEQ, HEADS * DH)
    attn_proj = jnp.dot(attended, out_proj, preferred_element_type=jnp.float32)
    residual = (inputs.astype(jnp.float32) + attn_proj).astype(jnp.bfloat16)
    moe_in = rms_scale(residual.astype(jnp.float32), moe_gain).astype(jnp.bfloat16)
    logits = jnp.dot(moe_in, router, preferred_element_type=jnp.float32)
    gate_vals = jax.nn.sigmoid(jnp.take_along_axis(logits, expert_ids, axis=1))
    flat_ids = expert_ids.reshape(-1)
    flat_gates = gate_vals.reshape(-1)
    most_rows = N_CTX * N_EXP * CAP

    def add_expert(expert_index, accum):
        matches = flat_ids == expert_index
        match_count = jnp.sum(matches.astype(jnp.int32))
        positions = jnp.nonzero(matches, size=most_rows, fill_value=0)[0].astype(jnp.int32)
        filled = jnp.arange(most_rows).astype(jnp.int32) < match_count
        token_ids = positions // TOPK
        row_vals = jnp.take(moe_in, token_ids, axis=0)
        w_gate = lax.dynamic_slice_in_dim(gate_proj, expert_index * FF, FF, 1)
        w_up = lax.dynamic_slice_in_dim(up_proj, expert_index * FF, FF, 1)
        w_down = lax.dynamic_slice_in_dim(down_proj, expert_index * FF, FF, 0)
        gate_act = jnp.dot(row_vals, w_gate, preferred_element_type=jnp.float32)
        up_act = jnp.dot(row_vals, w_up, preferred_element_type=jnp.float32)
        hidden = (jax.nn.silu(gate_act) * up_act).astype(jnp.bfloat16)
        out_rows = jnp.dot(hidden, w_down, preferred_element_type=jnp.float32).astype(jnp.bfloat16)
        weight = jnp.where(filled, jnp.take(flat_gates, positions), jnp.float32(0.0))
        return accum.at[token_ids].add(weight[:, None] * out_rows.astype(jnp.float32))
    moe_total = lax.fori_loop(0, EXPERTS, add_expert, jnp.zeros((SEQ, D), jnp.float32))
    return (residual.astype(jnp.float32) + moe_total).astype(jnp.bfloat16)
```

```python
import jax
import jax.numpy as jnp
from jax import lax
from jax.experimental import pallas as pl
from jax.experimental.pallas import tpu as pltpu
from jax.sharding import Mesh, PartitionSpec as P

BLK = 64
EPSILON = 1e-06


def rms_scale(values, gain_vec):
    mean_sq = jnp.mean(values * values, axis=-1, keepdims=True)
    return values * lax.rsqrt(mean_sq + EPSILON) * gain_vec


def attend_kernel(pos_ref, valid_ref, q_ref, kv_ref, o_ref, *, blocks, listed, span):
    scale = q_ref.shape[-1] ** (-0.5)
    width = listed * BLK
    row = lax.broadcasted_iota(jnp.int32, (BLK, width), 0)
    col = lax.broadcasted_iota(jnp.int32, (BLK, width), 1)
    causal = jnp.logical_or(col >= BLK, col <= row)
    which = col // BLK

    def one(n, carry):
        q = q_ref[pl.ds(pl.multiple_of(n * BLK, BLK), BLK), :]
        starts = [pl.multiple_of(pos_ref[n * listed + k], BLK) for k in range(listed)]
        keys = jnp.concatenate([kv_ref[pl.ds(s, BLK), :] for s in starts], axis=0)
        vals = jnp.concatenate([kv_ref[pl.ds(s + span, BLK), :] for s in starts], axis=0)
        scores = lax.dot_general(q, keys, (((1,), (1,)), ((), ())), preferred_element_type=jnp.float32)
        bits = jnp.full((BLK, width), valid_ref[n], jnp.int32)
        seen = jnp.logical_and(causal, ((bits >> which) & 1) == 1)
        p = jnp.where(seen, jnp.exp(scores * scale), jnp.float32(0.0))
        total = jnp.sum(p, axis=1, keepdims=True)
        acc = jnp.dot(p.astype(jnp.bfloat16), vals, preferred_element_type=jnp.float32)
        o_ref[pl.ds(pl.multiple_of(n * BLK, BLK), BLK), :] = (acc / total).astype(jnp.bfloat16)
        return carry

    lax.fori_loop(0, blocks, one, 0, unroll=2)


def attend(pos, valid, queries, kv):
    rows, dim = queries.shape
    blocks = rows // BLK
    listed = pos.shape[0] // blocks

    def kernel(pos_ref, valid_ref, q_ref, kv_ref, o_ref):
        attend_kernel(pos_ref, valid_ref, q_ref, kv_ref, o_ref, blocks=blocks, listed=listed, span=8 * BLK)

    smem = pl.BlockSpec(memory_space=pltpu.SMEM)
    vmem = pl.BlockSpec(memory_space=pltpu.VMEM)
    return pl.pallas_call(
        kernel,
        out_shape=jax.ShapeDtypeStruct((rows, dim), jnp.bfloat16),
        in_specs=[smem, smem, vmem, vmem],
        out_specs=vmem,
        name="attend",
    )(pos, valid, queries, kv)


def ring(size, step):
    return [(i, (i + step) % size) for i in range(size)]


def body(
    stored,
    depth_weights,
    attn_gain,
    qkv_proj,
    q_gain,
    k_gain,
    out_proj,
    moe_gain,
    router,
    gate_proj,
    up_proj,
    down_proj,
    expert_ids,
    block_pattern,
):
    bf16, f32 = jnp.bfloat16, jnp.float32
    nz, nx, ny = lax.axis_size("z"), lax.axis_size("x"), lax.axis_size("y")
    z, x, core, y = (lax.axis_index(a) for a in ("z", "x", "core", "y"))
    swap = [(0, 1), (1, 0)]
    depth_count, shard_len, feat_width = stored.shape

    half_rows = out_proj.shape[0] // 2
    own_half = lax.dynamic_slice_in_dim(out_proj, core * half_rows, half_rows, 0)
    o_lo = lax.ppermute(own_half, "y", ring(ny, 1))
    o_hi = lax.ppermute(own_half, "y", ring(ny, -1))
    quarter = half_rows // 2
    o_far0 = lax.ppermute(o_lo[:quarter], "y", ring(ny, 1))
    o_far1 = lax.ppermute(o_hi[quarter:], "y", ring(ny, -1))
    o_mine = jnp.concatenate([o_lo, o_hi, o_far0, o_far1], axis=0)
    o_other = lax.ppermute(o_mine, "core", swap)

    moves = []
    for y0 in range(0, ny, 2):
        moves += [(y0 + 1, y0), (ny + y0, ny + y0 + 1), (y0, ny + y0), (ny + y0 + 1, y0 + 1)]
    parts_a = [lax.ppermute(w, ("core", "y"), moves) for w in (gate_proj, up_proj, down_proj)]
    parts_b = [lax.ppermute(w, "core", swap) for w in parts_a]

    blended = depth_weights[0] * stored[0].astype(f32)
    for depth_step in range(1, depth_count):
        blended = blended + depth_weights[depth_step] * stored[depth_step].astype(f32)
    inputs = blended.astype(bf16)
    normed = rms_scale(inputs.astype(f32), attn_gain).astype(bf16)
    projected = jnp.einsum("td,dche->chte", normed, qkv_proj, preferred_element_type=f32)
    head_dim = projected.shape[3]
    queries = rms_scale(projected[0], q_gain[:, None, :]).astype(bf16)
    key_heads = rms_scale(projected[1], k_gain[:, None, :]).astype(bf16)
    value_heads = projected[2].astype(bf16)
    pair = jnp.stack([key_heads, value_heads], axis=1)
    pair = lax.all_to_all(pair, "z", split_axis=0, concat_axis=0, tiled=True)
    queries = lax.all_to_all(queries, "z", split_axis=0, concat_axis=0, tiled=True)
    kv_lo = lax.ppermute(pair, "x", ring(nx, 1))
    kv_hi = lax.ppermute(pair, "x", ring(nx, -1))
    kv_far0 = lax.ppermute(kv_lo[: nz // 2], "x", ring(nx, 1))
    kv_far1 = lax.ppermute(kv_hi[nz // 2 :], "x", ring(nx, -1))
    pieces = [pair, kv_lo, kv_hi, kv_far0, kv_far1]
    kv = jnp.concatenate(pieces + [lax.ppermute(p, "core", swap) for p in pieces], axis=0)
    kv = kv.reshape(-1, head_dim)

    own_head = y * nz + z
    per_shard = shard_len // BLK
    pattern = block_pattern.reshape(block_pattern.shape[0], nz, nx * 2, per_shard, -1)
    pattern = lax.dynamic_slice(
        pattern, (own_head, 0, x * 2 + core, 0, 0), (1, nz, 1, per_shard, pattern.shape[-1])
    )
    pattern = pattern.reshape(nz * per_shard, -1)
    bit = jnp.int32(1) << jnp.arange(pattern.shape[1], dtype=jnp.int32)
    valid = jnp.sum(jnp.where(pattern >= 0, bit[None, :], 0), axis=1)
    ids = jnp.maximum(pattern, 0)
    at_x = ((ids >> 4) - x) & 3
    at_x = jnp.where(at_x == 0, 0, jnp.where(at_x == 1, 2, jnp.where(at_x == 2, 3, 1)))
    piece = at_x + 4 * (((ids >> 3) & 1) ^ core)
    pos = ((piece * nz + (ids >> 6)) * 2 * per_shard + (ids & 7)) * BLK
    attended = attend(pos.reshape(-1), valid, queries.reshape(-1, head_dim), kv)

    tok_rows = shard_len // ny
    heads = lax.all_to_all(
        attended.reshape(nz * ny, tok_rows, head_dim), ("z", "y"), split_axis=0, concat_axis=0, tiled=True
    )
    heads = heads.reshape(nz, ny, tok_rows, head_dim)
    by_group = jnp.transpose(heads, (1, 2, 0, 3)).reshape(ny, tok_rows, nz * head_dim)

    def group(shift):
        return lax.dynamic_index_in_dim(by_group, (y + shift) % ny, 0, keepdims=False)

    def part(shift, which):
        return lax.dynamic_slice_in_dim(group(shift), which * half_rows, half_rows, 1)

    columns = [group(0)]
    for which in (core, 1 - core):
        columns += [part(-1, which), part(1, which), part(2, which)]
    o_all = jnp.concatenate([out_proj, o_mine, o_other], axis=0)
    attn_sum = jnp.dot(jnp.concatenate(columns, axis=1), o_all, preferred_element_type=f32)
    own_rows = lax.dynamic_slice_in_dim(inputs, y * tok_rows, tok_rows, 0)
    residual = (own_rows.astype(f32) + attn_sum).astype(bf16)

    devices = nz * nx * 2 * ny
    experts = devices // 2
    capacity = 8 * tok_rows // experts
    moe_in = rms_scale(residual.astype(f32), moe_gain).astype(bf16)
    logits = jnp.dot(moe_in, router, preferred_element_type=f32)
    choose = expert_ids[:, :, None] == jnp.arange(experts, dtype=jnp.int32)[None, None, :]
    picked = jnp.sum(jnp.where(choose, logits[:, None, :], f32(0.0)), axis=2)
    gate_vals = jax.nn.sigmoid(picked)
    hits = jnp.sum(choose.astype(jnp.int32), axis=1)
    before = jnp.cumsum(hits, axis=0) - hits
    slot = jnp.sum(jnp.where(choose, before[:, None, :], 0), axis=2)
    half_cap = capacity // 2
    chip_y = 2 * (expert_ids & 1) + ((expert_ids >> 1) & 1)
    device = (expert_ids >> 2) * (2 * ny) + (slot // half_cap) * ny + chip_y
    target = device * half_cap + slot % half_cap
    places = jnp.arange(experts * capacity, dtype=jnp.int32)
    placed = target[:, :, None] == places[None, None, :]
    dispatch = jnp.any(placed, axis=1).astype(bf16)
    send_rows = lax.dot_general(
        dispatch, moe_in, (((0,), (0,)), ((), ())), preferred_element_type=f32
    ).astype(bf16)
    everyone = ("z", "x", "core", "y")
    received = lax.all_to_all(
        send_rows.reshape(devices, half_cap, feat_width), everyone, split_axis=0, concat_axis=0, tiled=True
    )
    row_vals = received.reshape(-1, feat_width)
    value = None
    for w_gate, w_up, w_down in (parts_a, parts_b):
        gate_act = jnp.dot(row_vals, w_gate, preferred_element_type=f32)
        up_act = jnp.dot(row_vals, w_up, preferred_element_type=f32)
        hidden = (jax.nn.silu(gate_act) * up_act).astype(bf16)
        term = jnp.dot(hidden, w_down, preferred_element_type=f32)
        value = term if value is None else value + term
    returned = lax.all_to_all(
        value.astype(bf16).reshape(devices, half_cap, feat_width),
        everyone,
        split_axis=0,
        concat_axis=0,
        tiled=True,
    ).reshape(-1, feat_width)
    weight = jnp.sum(jnp.where(placed, gate_vals[:, :, None], f32(0.0)), axis=1)
    high = weight.astype(bf16)
    low = (weight - high.astype(f32)).astype(bf16)
    both = jnp.dot(jnp.concatenate([high, low], axis=0), returned, preferred_element_type=f32)
    moe_out = both[:tok_rows] + both[tok_rows:]
    return (residual.astype(f32) + moe_out).astype(bf16)


def solution(mesh):
    devices = mesh.devices
    ny = devices.shape[1]
    cube = Mesh(devices.reshape(ny, devices.shape[0] // (2 * ny), 2, ny), ("z", "x", "core", "y"))
    ctx = ("z", "x", "core")
    every = ("z", "x", "core", "y")
    return jax.shard_map(
        body,
        mesh=cube,
        in_specs=(
            P(None, ctx, None),
            P(),
            P(),
            P(None, None, "y", None),
            P("y", None),
            P("y", None),
            P("y", None),
            P(),
            P(),
            P(None, every),
            P(None, every),
            P(every, None),
            P(every, None),
            P(),
        ),
        out_specs=P(every, None),
        check_vma=False,
    )
```
